32 devices in a mesh: dom: 4 (over z), blk: 8 (over y, x, core).
Axes of the slice: x: 2, y: 2, z: 4, core: 2. Of those that a mesh axis runs over, the one named last changes fastest.
Arguments:
- features: bfloat16 [16384, 128], P(('dom', 'blk')), may hold values from -6 to 6
- history: bfloat16 [16384, 512], P(('dom', 'blk')), may hold values from 0 to 1.5
- adj_tiles: bfloat16 [16384, 4, 512], P(('dom', 'blk')), may hold values from -0.109375 to 0.109375
- tile_cols: int32 [4, 8, 4], P('dom', 'blk'), may hold values from 0 to 7, as said below
- bound_one: bfloat16 [16384, 1024], P(('dom', 'blk')), may hold values from -0.109375 to 0.109375
- bound_two: bfloat16 [16384, 1024], P(('dom', 'blk')), may hold values from -0.109375 to 0.109375
- block_ids: int32 [2, 4, 8, 4, 2], P(None, 'dom', 'blk'), may hold values from 0 to 3
- block_counts: int32 [2, 4, 8, 4], P(None, 'dom', 'blk'), may hold values from 0 to 2, as said below
- w_in: bfloat16 [128, 512], replicated, may hold values from -0.5 to 0.5
- b_in: float32 [512], replicated, may hold values from -3 to 3
- w_out: bfloat16 [512, 512], replicated, may hold values from -0.25 to 0.25
- b_out: float32 [512], replicated, may hold values from -3 to 3
Outputs:
- fresh_history: bfloat16 [16384, 512], P(('dom', 'blk'))
- node_out: bfloat16 [16384, 512], P(('dom', 'blk'))
The draws below stay inside these ranges and needn't reach their ends.
Inputs may be any that keep to these rules, and one draw needn't show every extreme that they name: `tile_cols`: each device's list names 4 distinct blk indices, its own first. `block_counts`: zero where owner and reader are the same partition; for every layer and reader partition some blk index receives 2 live slots from every other partition.
All inputs are finite; a program needn't handle non-finite values.
Results may differ from the reference program's by a relative error of at most 0.0055.
Values may be sent and summed in bfloat16 or wider, within the bound.
No kernel may reach another device: no remote copies, remote signals or barrier semaphores. Data moves between devices by JAX's collectives and lax.ppermute only.
A program may use at most 64 MiB of HBM per device.

```python
import jax
import jax.numpy as jnp
from jax import lax

IN_WIDTH = 128
WIDTH = 512
ROWS = 512
BLOCK = 128
SLOTS = 2
BLOCKS_DEV = 4
OCCUPIED = 4
BORDER = 1024
NODES = 16384
N_DOM = 4
N_BLK = 8


def draw_tile_cols(key, part):
    device_count = N_DOM * N_BLK
    row_keys = jax.random.split(key, device_count)
    shuffled = jax.vmap(lambda row_key: jax.random.permutation(row_key, N_BLK - 1))(row_keys)
    offsets = jnp.concatenate([jnp.zeros((device_count, 1), jnp.int32), shuffled[:, :OCCUPIED - 1].astype(jnp.int32) + 1], axis=1)
    own_index = jnp.arange(device_count, dtype=jnp.int32) % N_BLK
    return ((own_index[:, None] + offsets) % N_BLK).reshape(N_DOM, N_BLK, OCCUPIED).astype(jnp.int32)


def draw_block_counts(key, part):
    first_key = jax.random.fold_in(key, 11)
    second_key = jax.random.fold_in(key, 23)
    base_counts = jax.random.randint(first_key, (2, N_DOM, N_BLK, N_DOM), 0, SLOTS + 1)
    busy_reader = jax.random.randint(second_key, (2, 1, 1, N_DOM), 0, N_BLK)
    group_index = jnp.arange(N_BLK, dtype=jnp.int32)[None, None, :, None]
    base_counts = jnp.where(group_index == busy_reader, SLOTS, base_counts)
    owner_index = jnp.arange(N_DOM, dtype=jnp.int32)[None, :, None, None]
    reader_index = jnp.arange(N_DOM, dtype=jnp.int32)[None, None, None, :]
    return jnp.where(owner_index == reader_index, 0, base_counts).astype(jnp.int32)


def set_ends(result, rng, least, top_value):
    spot = [jax.random.randint(jax.random.fold_in(rng, axis), (), 0, length) for axis, length in enumerate(result.shape)]
    longest = result.shape.index(max(result.shape))
    neighbour = spot[:longest] + [(spot[longest] + 1) % result.shape[longest]] + spot[longest + 1:]
    return result.at[tuple(spot)].set(least).at[tuple(neighbour)].set(top_value)


def level_of(rng, dims, cuts, smallest, top_value):
    gain, own = 1.0, jax.random.fold_in(rng, 6)
    for axis_at, blocks in cuts:
        steps = jnp.exp(jax.random.uniform(jax.random.fold_in(own, axis_at), (blocks,), jnp.float32, smallest / len(cuts), top_value / len(cuts)))
        gain = gain * jnp.repeat(steps, dims[axis_at] // blocks).reshape([-1 if axis == axis_at else 1 for axis in range(len(dims))])
    return gain


def centred(stream_key, dims, deviation, limit, shards=(), kind=jnp.bfloat16):
    factor_of = level_of(stream_key, dims, shards, -0.22, 0.18) if shards else 1.0
    drawn = jax.random.normal(stream_key, dims, jnp.float32) * deviation * factor_of
    return jnp.minimum(jnp.maximum(drawn, -limit), limit).astype(kind)


def setup_inputs(seed: int = 0) -> dict:
    seeds = jax.random.split(jax.random.key(seed), 13)
    return {
        "features": centred(seeds[0], (NODES, IN_WIDTH), 1.0, 6.0, ((0, 32),)),
        "history": jnp.clip(1.5 * jax.random.uniform(seeds[1], (NODES, WIDTH), jnp.float32) ** level_of(seeds[1], (NODES, WIDTH), ((0, 32),), -0.2, 0.2), 0.0, 1.5).astype(jnp.bfloat16),
        "adj_tiles": centred(seeds[2], (NODES, OCCUPIED, ROWS), (OCCUPIED * ROWS + BORDER) ** -0.5, 0.109375, ((0, 32),)),
        "tile_cols": draw_tile_cols(jax.random.fold_in(seeds[12], 71), 0),
        "bound_one": centred(seeds[4], (NODES, BORDER), (OCCUPIED * ROWS + BORDER) ** -0.5, 0.109375, ((0, 32),)),
        "bound_two": centred(seeds[5], (NODES, BORDER), (OCCUPIED * ROWS + BORDER) ** -0.5, 0.109375, ((0, 32),)),
        "block_ids": set_ends(jax.random.randint(seeds[6], (2, N_DOM, N_BLK, N_DOM, SLOTS), 0, BLOCKS_DEV), jax.random.fold_in(seeds[6], 1), 0, BLOCKS_DEV - 1).astype(jnp.int32),
        "block_counts": draw_block_counts(jax.random.fold_in(seeds[12], 71), 0),
        "w_in": centred(seeds[8], (IN_WIDTH, WIDTH), IN_WIDTH ** -0.5, 0.5),
        "b_in": centred(seeds[9], (WIDTH,), 0.5, 3.0, (), jnp.float32),
        "w_out": centred(seeds[10], (WIDTH, WIDTH), WIDTH ** -0.5, 0.25),
        "b_out": centred(seeds[11], (WIDTH,), 0.5, 3.0, (), jnp.float32),
    }


def border_rows_of(source_panel, block_ids, block_counts, layer_index):
    width = source_panel.shape[1]
    blocks = source_panel.reshape(N_DOM, N_BLK, BLOCKS_DEV, BLOCK, width)
    owner_index = jnp.arange(N_DOM, dtype=jnp.int32)[:, None, None, None]
    group_index = jnp.arange(N_BLK, dtype=jnp.int32)[None, :, None, None]
    picked = blocks[owner_index, group_index, block_ids[layer_index].astype(jnp.int32)]
    slot_index = jnp.arange(SLOTS, dtype=jnp.int32)[None, None, None, :]
    is_live = slot_index < block_counts[layer_index][..., None]
    picked = jnp.where(is_live[..., None, None], picked, jnp.zeros((), picked.dtype))
    return picked.transpose(2, 1, 0, 3, 4, 5).reshape(N_DOM * N_BLK, BORDER, width)


def aggregate(row_panels, received, adj_tiles, tile_cols, bound):
    width = row_panels.shape[1]
    panels = row_panels.reshape(N_DOM, N_BLK, ROWS, width)
    device_count = N_DOM * N_BLK
    tiles = adj_tiles.reshape(device_count, ROWS, OCCUPIED * ROWS)
    columns = tile_cols.reshape(device_count, OCCUPIED).astype(jnp.int32)
    border = bound.reshape(device_count, ROWS, BORDER)

    def device_rows(pieces):
        device, tile_rows, column_list, border_rows, border_feats = pieces
        stacked = panels[device // N_BLK][column_list].reshape(OCCUPIED * ROWS, width)
        inside = jnp.dot(tile_rows, stacked, preferred_element_type=jnp.float32)
        outside = jnp.dot(border_rows, border_feats, preferred_element_type=jnp.float32)
        return (inside + outside).astype(jnp.bfloat16)

    device_list = jnp.arange(device_count, dtype=jnp.int32)
    merged = lax.map(device_rows, (device_list, tiles, columns, border, received))
    return merged.reshape(NODES, width)


def reference(features, history, adj_tiles, tile_cols, bound_one, bound_two, block_ids, block_counts, w_in, b_in, w_out, b_out):
    received_one = border_rows_of(features, block_ids, block_counts, 0)
    first_agg = aggregate(features, received_one, adj_tiles, tile_cols, bound_one)
    first_pre = jnp.dot(first_agg, w_in, preferred_element_type=jnp.float32) + b_in
    fresh_history = jnp.maximum(first_pre, 0.0).astype(jnp.bfloat16)
    received_two = border_rows_of(history, block_ids, block_counts, 1)
    second_agg = aggregate(fresh_history, received_two, adj_tiles, tile_cols, bound_two)
    node_out = (jnp.dot(second_agg, w_out, preferred_element_type=jnp.float32) + b_out).astype(jnp.bfloat16)
    return (fresh_history, node_out)
```

```python
import functools

import jax
import jax.numpy as jnp
from jax import lax
from jax.experimental import pallas as pl
from jax.experimental.pallas import tpu as pltpu
from jax.sharding import PartitionSpec as P


BF16 = jnp.bfloat16
F32 = jnp.float32
VMEM = pl.BlockSpec(memory_space=pltpu.VMEM)
SMEM = pl.BlockSpec(memory_space=pltpu.SMEM)


def dot(a, b):
    return jnp.dot(a, b, preferred_element_type=F32)


def pack_kernel(layer, place_ref, ids_ref, counts_ref, panel_ref, *out_refs):
    n_dom, slots = ids_ref.shape[-2:]
    rows = out_refs[0].shape[0] // slots
    dom = place_ref[0]
    for shift, out_ref in enumerate(out_refs, 1):
        reader = lax.rem(dom + shift, n_dom)
        live = counts_ref[layer, 0, 0, reader]
        for slot in range(slots):
            start = pl.multiple_of(ids_ref[layer, 0, 0, reader, slot] * rows, rows)
            here = pl.ds(slot * rows, rows)

            @pl.when(slot < live)
            def _():
                out_ref[here, :] = panel_ref[pl.ds(start, rows), :]

            @pl.when(slot >= live)
            def _():
                out_ref[here, :] = jnp.zeros((rows, out_ref.shape[1]), out_ref.dtype)


def pack(layer, place, ids, counts, panel, slot_rows):
    n_dom = ids.shape[-2]
    return pl.pallas_call(
        functools.partial(pack_kernel, layer),
        out_shape=[jax.ShapeDtypeStruct((slot_rows, panel.shape[1]), panel.dtype)] * (n_dom - 1),
        in_specs=[SMEM, SMEM, SMEM, VMEM],
        out_specs=[VMEM] * (n_dom - 1),
        name=f"pack{layer}",
    )(place, ids, counts, panel)


def pick_panels(blk, cols_ref, panel_refs, chosen_ref):
    occupied = cols_ref.shape[-1]
    chosen_ref[0] = panel_refs[0][...]
    for k in range(1, occupied):
        apart = lax.bitwise_xor(cols_ref[0, 0, k], blk)
        for d, panel_ref in enumerate(panel_refs):
            @pl.when(apart == d)
            def _():
                chosen_ref[k] = panel_ref[...]


def border_product(dom, bound_ref, border_refs, shifts):
    n_dom = bound_ref.shape[1] // border_refs[0].shape[0]
    total = None
    for border_ref, shift in zip(border_refs, shifts):
        width = border_ref.shape[0]
        owner = lax.rem(dom + n_dom - shift, n_dom)
        part = dot(bound_ref[:, pl.ds(pl.multiple_of(owner * width, width), width)], border_ref[...])
        total = part if total is None else total + part
    return total


def first_kernel(n_blk, place_ref, cols_ref, tiles_ref, bound_ref, *refs):
    panel_refs, border_refs = refs[:n_blk], refs[n_blk:-2]
    agg_ref, chosen_ref = refs[-2:]
    pick_panels(place_ref[1], cols_ref, panel_refs, chosen_ref)
    total = border_product(place_ref[0], bound_ref, border_refs, range(1, len(border_refs) + 1))
    for k in range(cols_ref.shape[-1]):
        total = total + dot(tiles_ref[k], chosen_ref[k])
    agg_ref[...] = total.astype(BF16)


def first_layer(place, cols, tiles, bound, panels, border):
    shape = panels[0].shape
    return pl.pallas_call(
        functools.partial(first_kernel, len(panels)),
        out_shape=jax.ShapeDtypeStruct(shape, BF16),
        in_specs=[SMEM, SMEM] + [VMEM] * (2 + len(panels) + len(border)),
        out_specs=VMEM,
        scratch_shapes=[pltpu.VMEM((cols.shape[-1],) + shape, BF16)],
        name="first",
    )(place, cols, tiles, bound, *panels, *border)


def inside_kernel(n_blk, place_ref, cols_ref, tiles_ref, w_ref, b_ref, *refs):
    panel_refs = refs[:n_blk]
    fresh_ref, total_ref, chosen_ref = refs[n_blk:]
    pick_panels(place_ref[1], cols_ref, panel_refs, chosen_ref)
    total = None
    for k in range(cols_ref.shape[-1]):
        fresh = jnp.maximum(dot(chosen_ref[k], w_ref[...]) + b_ref[...], 0.0).astype(BF16)
        if k == 0:
            fresh_ref[...] = fresh
        part = dot(tiles_ref[k], fresh)
        total = part if total is None else total + part
    total_ref[...] = total


def inside(place, cols, tiles, w_in, b_in, panels):
    shape = panels[0].shape
    rows, width = shape[0], w_in.shape[1]
    return pl.pallas_call(
        functools.partial(inside_kernel, len(panels)),
        out_shape=[jax.ShapeDtypeStruct((rows, width), BF16), jax.ShapeDtypeStruct((rows, width), F32)],
        in_specs=[SMEM, SMEM] + [VMEM] * (3 + len(panels)),
        out_specs=[VMEM, VMEM],
        scratch_shapes=[pltpu.VMEM((cols.shape[-1],) + shape, BF16)],
        name="inside",
    )(place, cols, tiles, w_in, b_in, *panels)


def last_kernel(place_ref, total_ref, bound_ref, w_ref, b_ref, *refs):
    border_refs, out_ref = refs[:-1], refs[-1]
    total = total_ref[...] + border_product(place_ref[0], bound_ref, border_refs, range(1, len(border_refs) + 1))
    out_ref[...] = (dot(total.astype(BF16), w_ref[...]) + b_ref[...]).astype(BF16)


def last_layer(place, total, bound, w_out, b_out, border):
    return pl.pallas_call(
        last_kernel,
        out_shape=jax.ShapeDtypeStruct((total.shape[0], w_out.shape[1]), BF16),
        in_specs=[SMEM] + [VMEM] * (4 + len(border)),
        out_specs=VMEM,
        name="last",
    )(place, total, bound, w_out, b_out, *border)


def swap(block, apart):
    n_blk = lax.axis_size("blk")
    return lax.ppermute(block, "blk", [(i, i ^ apart) for i in range(n_blk)])


def send_on(block, shift):
    n_dom = lax.axis_size("dom")
    return lax.ppermute(block, "dom", [(i, (i + shift) % n_dom) for i in range(n_dom)])


def all_panels(panel):
    n_blk = lax.axis_size("blk")
    panels = {0: panel}
    far = sorted(range(2, n_blk, 2), key=lambda d: -bin(d).count("1"))
    for d in far:
        panels[d] = swap(panel, d)
    panels[1] = swap(panel, 1)
    for d in far:
        panels[d + 1] = swap(panels[d], 1)
    return [panels[d] for d in range(n_blk)]


def body(features, history, adj_tiles, tile_cols, bound_one, bound_two, block_ids, block_counts, w_in, b_in, w_out, b_out):
    n_dom = lax.axis_size("dom")
    slot_rows = bound_one.shape[1] // n_dom
    place = jnp.stack([lax.axis_index("dom"), lax.axis_index("blk")]).astype(jnp.int32)
    out_one = pack(0, place, block_ids, block_counts, features, slot_rows)
    border_one = [send_on(block, s) for s, block in enumerate(out_one, 1)]
    panels_one = all_panels(features)
    out_two = pack(1, place, block_ids, block_counts, history, slot_rows)
    border_two = [send_on(block, s) for s, block in enumerate(out_two, 1)]
    tiles = adj_tiles.transpose(1, 0, 2)
    agg = first_layer(place, tile_cols, tiles, bound_one, panels_one, border_one)
    panels_two = all_panels(agg)
    fresh, total = inside(place, tile_cols, tiles, w_in, b_in.reshape(1, -1), panels_two)
    out = last_layer(place, total, bound_two, w_out, b_out.reshape(1, -1), border_two)
    return fresh, out


def solution(mesh):
    rows = P(("dom", "blk"), None)
    placed = (
        rows,
        rows,
        P(("dom", "blk"), None, None),
        P("dom", "blk", None),
        rows,
        rows,
        P(None, "dom", "blk", None, None),
        P(None, "dom", "blk", None),
        P(),
        P(),
        P(),
        P(),
    )
    return jax.shard_map(body, mesh=mesh, in_specs=placed, out_specs=(rows, rows), check_vma=False)
```

```python
import functools

import jax
import jax.numpy as jnp
from jax import lax
from jax.experimental import pallas as pl
from jax.experimental.pallas import tpu as pltpu
from jax.sharding import PartitionSpec as P


BF16 = jnp.bfloat16
F32 = jnp.float32
VMEM = pl.BlockSpec(memory_space=pltpu.VMEM)
MIB = 1 << 20
SMEM = pl.BlockSpec(memory_space=pltpu.SMEM)


def near(array):
    return pltpu.with_memory_space_constraint(array, pltpu.VMEM)


def dot(a, b):
    return jnp.dot(a, b, preferred_element_type=F32)


def pack_kernel(layer, ids_ref, counts_ref, panel_ref, *out_refs):
    slots, n_dom = ids_ref.shape[-2:]
    rows = out_refs[0].shape[0] // slots
    dom = lax.axis_index("dom")
    for shift, out_ref in enumerate(out_refs, 1):
        reader = lax.rem(dom + shift, n_dom)
        live = counts_ref[layer, 0, 0, reader]
        for slot in range(slots):
            start = pl.multiple_of(ids_ref[layer, 0, 0, slot, reader] * rows, rows)
            here = pl.ds(slot * rows, rows)

            @pl.when(slot < live)
            def _():
                out_ref[here, :] = panel_ref[pl.ds(start, rows), :]

            @pl.when(slot >= live)
            def _():
                out_ref[here, :] = jnp.zeros((rows, out_ref.shape[1]), out_ref.dtype)


def pack(layer, ids, counts, panel, slot_rows):
    n_dom = ids.shape[-1]
    return pl.pallas_call(
        functools.partial(pack_kernel, layer),
        out_shape=[pltpu.VMEM((slot_rows, panel.shape[1]), panel.dtype)] * (n_dom - 1),
        in_specs=[SMEM, SMEM, VMEM],
        out_specs=[VMEM] * (n_dom - 1),
        compiler_params=pltpu.CompilerParams(vmem_limit_bytes=MIB),
    )(ids, counts, near(panel))


def pick_panels(blk, cols_ref, panel_refs, chosen_ref):
    occupied = cols_ref.shape[-1]
    chosen_ref[0] = panel_refs[0][...]
    for k in range(1, occupied):
        apart = lax.bitwise_xor(cols_ref[0, 0, k], blk)
        for d, panel_ref in enumerate(panel_refs):
            @pl.when(apart == d)
            def _():
                chosen_ref[k] = panel_ref[...]


def border_product(dom, bound_ref, border_refs, shifts):
    n_dom = bound_ref.shape[1] // border_refs[0].shape[0]
    total = None
    for border_ref, shift in zip(border_refs, shifts):
        width = border_ref.shape[0]
        owner = lax.rem(dom + n_dom - shift, n_dom)
        part = dot(bound_ref[:, pl.ds(pl.multiple_of(owner * width, width), width)], border_ref[...])
        total = part if total is None else total + part
    return total


def first_kernel(n_blk, cols_ref, tiles_ref, bound_ref, *refs):
    panel_refs, border_refs = refs[:n_blk], refs[n_blk:-2]
    agg_ref, chosen_ref = refs[-2:]
    pick_panels(lax.axis_index("blk"), cols_ref, panel_refs, chosen_ref)
    total = border_product(lax.axis_index("dom"), bound_ref, border_refs, range(1, len(border_refs) + 1))
    for k in range(cols_ref.shape[-1]):
        total = total + dot(tiles_ref[k], chosen_ref[k])
    agg_ref[...] = total.astype(BF16)


def first_layer(cols, tiles, bound, panels, border):
    shape = panels[0].shape
    return pl.pallas_call(
        functools.partial(first_kernel, len(panels)),
        out_shape=pltpu.VMEM(shape, BF16),
        in_specs=[SMEM] + [VMEM] * (2 + len(panels) + len(border)),
        out_specs=VMEM,
        scratch_shapes=[pltpu.VMEM((cols.shape[-1],) + shape, BF16)],
        compiler_params=pltpu.CompilerParams(vmem_limit_bytes=8 * MIB),
        name="first",
    )(cols, *map(near, (tiles, bound, *panels, *border)))


def inside_kernel(n_blk, cols_ref, tiles_ref, w_ref, b_ref, *refs):
    panel_refs = refs[:n_blk]
    fresh_ref, total_ref, chosen_ref = refs[n_blk:]
    pick_panels(lax.axis_index("blk"), cols_ref, panel_refs, chosen_ref)
    total = None
    for k in range(cols_ref.shape[-1]):
        fresh = jnp.maximum(dot(chosen_ref[k], w_ref[...]) + b_ref[...], 0.0).astype(BF16)
        if k == 0:
            fresh_ref[...] = fresh
        part = dot(tiles_ref[k], fresh)
        total = part if total is None else total + part
    total_ref[...] = total


def inside(cols, tiles, w_in, b_in, panels):
    shape = panels[0].shape
    rows, width = shape[0], w_in.shape[1]
    return pl.pallas_call(
        functools.partial(inside_kernel, len(panels)),
        out_shape=[jax.ShapeDtypeStruct((rows, width), BF16), pltpu.VMEM((rows, width), F32)],
        in_specs=[SMEM] + [VMEM] * (3 + len(panels)),
        out_specs=[VMEM, VMEM],
        scratch_shapes=[pltpu.VMEM((cols.shape[-1],) + shape, BF16)],
        compiler_params=pltpu.CompilerParams(vmem_limit_bytes=12 * MIB),
        name="inside",
    )(cols, *map(near, (tiles, w_in, b_in, *panels)))


def last_kernel(total_ref, bound_ref, w_ref, b_ref, *refs):
    border_refs, out_ref = refs[:-1], refs[-1]
    total = total_ref[...] + border_product(lax.axis_index("dom"), bound_ref, border_refs, range(1, len(border_refs) + 1))
    out_ref[...] = (dot(total.astype(BF16), w_ref[...]) + b_ref[...]).astype(BF16)


def last_layer(total, bound, w_out, b_out, border):
    return pl.pallas_call(
        last_kernel,
        out_shape=jax.ShapeDtypeStruct((total.shape[0], w_out.shape[1]), BF16),
        in_specs=[VMEM] * (4 + len(border)),
        out_specs=VMEM,
        compiler_params=pltpu.CompilerParams(vmem_limit_bytes=8 * MIB),
        name="last",
    )(*map(near, (total, bound, w_out, b_out, *border)))


def swap(block, apart):
    n_blk = lax.axis_size("blk")
    return lax.ppermute(block, "blk", [(i, i ^ apart) for i in range(n_blk)])


def send_on(block, shift):
    n_dom = lax.axis_size("dom")
    return lax.ppermute(block, "dom", [(i, (i + shift) % n_dom) for i in range(n_dom)])


def all_panels(panel):
    n_blk = lax.axis_size("blk")
    panels = {0: panel}
    far = sorted(range(2, n_blk, 2), key=lambda d: -bin(d).count("1"))
    for d in far:
        panels[d] = swap(panel, d)
    panels[1] = swap(panel, 1)
    for d in far:
        panels[d + 1] = swap(panels[d], 1)
    return [panels[d] for d in range(n_blk)]


def borders(layer, ids, counts, panel, slot_rows):
    blocks = pack(layer, ids, counts, panel, slot_rows)
    return [send_on(block, s) for s, block in enumerate(blocks, 1)]


def body(features, history, adj_tiles, tile_cols, bound_one, bound_two, block_ids, block_counts, w_in, b_in, w_out, b_out):
    slot_rows = bound_one.shape[1] // lax.axis_size("dom")
    ids = block_ids.swapaxes(3, 4)
    panels_one = all_panels(features)
    border_one = borders(0, ids, block_counts, features, slot_rows)
    border_two = borders(1, ids, block_counts, history, slot_rows)
    tiles = adj_tiles.transpose(1, 0, 2)
    agg = first_layer(tile_cols, tiles, bound_one, panels_one, border_one)
    panels_two = all_panels(agg)
    fresh, total = inside(tile_cols, tiles, w_in, b_in.reshape(1, -1), panels_two)
    out = last_layer(total, bound_two, w_out, b_out.reshape(1, -1), border_two)
    return fresh, out


def solution(mesh):
    rows = P(("dom", "blk"), None)
    placed = (
        rows,
        rows,
        P(("dom", "blk"), None, None),
        P("dom", "blk", None),
        rows,
        rows,
        P(None, "dom", "blk", None, None),
        P(None, "dom", "blk", None),
        P(),
        P(),
        P(),
        P(),
    )
    return jax.shard_map(body, mesh=mesh, in_specs=placed, out_specs=(rows, rows), check_vma=False)
```

```python
import functools

import jax
import jax.numpy as jnp
from jax import lax
from jax.experimental import pallas as pl
from jax.experimental.pallas import tpu as pltpu
from jax.sharding import PartitionSpec as P


BF16 = jnp.bfloat16
F32 = jnp.float32
VMEM = pl.BlockSpec(memory_space=pltpu.VMEM)
MIB = 1 << 20
SMEM = pl.BlockSpec(memory_space=pltpu.SMEM)


def far(array):
    return pltpu.with_memory_space_constraint(array, pltpu.HBM)


def near(array):
    return pltpu.with_memory_space_constraint(array, pltpu.VMEM)


def dot(a, b):
    return jnp.dot(a, b, preferred_element_type=F32)


def pack_kernel(*refs):
    layers, slots, n_dom = refs[0].shape[0], *refs[0].shape[-2:]
    came_refs = refs[:layers + 2]
    out_refs = refs[layers + 2:-layers - 3]
    held_refs, sems = refs[-layers - 3:-1], refs[-1]
    ids_ref, counts_ref, *panel_refs = held_refs
    copies = [pltpu.make_async_copy(*pair, sems.at[n]) for n, pair in enumerate(zip(came_refs, held_refs))]
    for copy in copies:
        copy.start()
    copies[0].wait()
    copies[1].wait()
    dom = lax.axis_index("dom")
    for layer in range(layers):
        copies[2 + layer].wait()
        for apart in range(1, n_dom):
            out_ref = out_refs[layer * (n_dom - 1) + apart - 1]
            rows, width = out_ref.shape[0] // slots, out_ref.shape[1]
            reader = lax.bitwise_xor(dom, apart)
            live = counts_ref[layer, 0, 0, reader]
            for slot in range(slots):
                start = pl.multiple_of(ids_ref[layer, 0, 0, slot, reader] * rows, rows)
                here = pl.ds(slot * rows, rows)

                @pl.when(slot < live)
                def _():
                    out_ref[here, :] = panel_refs[layer][pl.ds(start, rows), :]

                @pl.when(slot >= live)
                def _():
                    out_ref[here, :] = jnp.zeros((rows, width), out_ref.dtype)


def pack(ids, counts, panels, slot_rows):
    n_dom = ids.shape[-1]
    blocks = pl.pallas_call(
        pack_kernel,
        out_shape=[pltpu.VMEM((slot_rows, panel.shape[1]), panel.dtype) for panel in panels for _ in range(n_dom - 1)],
        in_specs=[pl.BlockSpec(memory_space=pltpu.HBM)] * (2 + len(panels)),
        out_specs=[VMEM] * (len(panels) * (n_dom - 1)),
        scratch_shapes=[pltpu.SMEM(a.shape, a.dtype) for a in (ids, counts)]
        + [pltpu.VMEM(panel.shape, panel.dtype) for panel in panels]
        + [pltpu.SemaphoreType.DMA((2 + len(panels),))],
        compiler_params=pltpu.CompilerParams(vmem_limit_bytes=2 * MIB),
        name="pack",
    )(*map(far, (ids, counts, *panels)))
    return [blocks[n * (n_dom - 1):(n + 1) * (n_dom - 1)] for n in range(len(panels))]


def pick_panels(blk, cols_ref, panel_refs, chosen_ref):
    occupied = cols_ref.shape[-1]
    chosen_ref[0] = panel_refs[0][...]
    for k in range(1, occupied):
        apart = lax.bitwise_xor(cols_ref[0, 0, k], blk)
        for d, panel_ref in enumerate(panel_refs):
            @pl.when(apart == d)
            def _():
                chosen_ref[k] = panel_ref[...]


def border_product(dom, bound_ref, border_refs, distances):
    total = None
    for border_ref, apart in zip(border_refs, distances):
        width = border_ref.shape[0]
        owner = lax.bitwise_xor(dom, apart)
        part = dot(bound_ref[:, pl.ds(pl.multiple_of(owner * width, width), width)], border_ref[...])
        total = part if total is None else total + part
    return total


def first_kernel(n_blk, cols_ref, tiles_ref, bound_ref, *refs):
    panel_refs, border_refs = refs[:n_blk], refs[n_blk:-2]
    agg_ref, chosen_ref = refs[-2:]
    pick_panels(lax.axis_index("blk"), cols_ref, panel_refs, chosen_ref)
    total = border_product(lax.axis_index("dom"), bound_ref, border_refs, range(1, len(border_refs) + 1))
    for k in range(cols_ref.shape[-1]):
        total = total + dot(tiles_ref[k], chosen_ref[k])
    agg_ref[...] = total.astype(BF16)


def first_layer(cols, tiles, bound, panels, border):
    shape = panels[0].shape
    return pl.pallas_call(
        functools.partial(first_kernel, len(panels)),
        out_shape=pltpu.VMEM(shape, BF16),
        in_specs=[SMEM] + [VMEM] * (2 + len(panels) + len(border)),
        out_specs=VMEM,
        scratch_shapes=[pltpu.VMEM((cols.shape[-1],) + shape, BF16)],
        compiler_params=pltpu.CompilerParams(vmem_limit_bytes=8 * MIB),
        name="first",
    )(cols, *map(near, (tiles, bound, *panels, *border)))


def inside_kernel(n_blk, cols_ref, tiles_ref, w_ref, b_ref, *refs):
    panel_refs = refs[:n_blk]
    fresh_ref, total_ref, chosen_ref = refs[n_blk:]
    pick_panels(lax.axis_index("blk"), cols_ref, panel_refs, chosen_ref)
    total = None
    for k in range(cols_ref.shape[-1]):
        fresh = jnp.maximum(dot(chosen_ref[k], w_ref[...]) + b_ref[...], 0.0).astype(BF16)
        if k == 0:
            fresh_ref[...] = fresh
        part = dot(tiles_ref[k], fresh)
        total = part if total is None else total + part
    total_ref[...] = total


def inside(cols, tiles, w_in, b_in, panels):
    shape = panels[0].shape
    rows, width = shape[0], w_in.shape[1]
    return pl.pallas_call(
        functools.partial(inside_kernel, len(panels)),
        out_shape=[jax.ShapeDtypeStruct((rows, width), BF16), pltpu.VMEM((rows, width), F32)],
        in_specs=[SMEM] + [VMEM] * (3 + len(panels)),
        out_specs=[VMEM, VMEM],
        scratch_shapes=[pltpu.VMEM((cols.shape[-1],) + shape, BF16)],
        compiler_params=pltpu.CompilerParams(vmem_limit_bytes=12 * MIB),
        name="inside",
    )(cols, *map(near, (tiles, w_in, b_in, *panels)))


def last_kernel(total_ref, bound_ref, w_ref, b_ref, *refs):
    border_refs, out_ref = refs[:-1], refs[-1]
    total = total_ref[...] + border_product(lax.axis_index("dom"), bound_ref, border_refs, range(1, len(border_refs) + 1))
    out_ref[...] = (dot(total.astype(BF16), w_ref[...]) + b_ref[...]).astype(BF16)


def last_layer(total, bound, w_out, b_out, border):
    return pl.pallas_call(
        last_kernel,
        out_shape=jax.ShapeDtypeStruct((total.shape[0], w_out.shape[1]), BF16),
        in_specs=[VMEM] * (4 + len(border)),
        out_specs=VMEM,
        compiler_params=pltpu.CompilerParams(vmem_limit_bytes=8 * MIB),
        name="last",
    )(*map(near, (total, bound, w_out, b_out, *border)))


def swap(block, axis, apart):
    return lax.ppermute(block, axis, [(i, i ^ apart) for i in range(lax.axis_size(axis))])


def all_panels(panel):
    n_blk = lax.axis_size("blk")
    panels = {0: panel}
    far = sorted(range(2, n_blk, 2), key=lambda d: -bin(d).count("1"))
    for d in far:
        panels[d] = swap(panel, "blk", d)
    panels[1] = swap(panel, "blk", 1)
    for d in far:
        panels[d + 1] = swap(panels[d], "blk", 1)
    return [panels[d] for d in range(n_blk)]


def borders(blocks):
    return [swap(block, "dom", apart) for apart, block in enumerate(blocks, 1)]


def body(features, history, adj_tiles, tile_cols, bound_one, bound_two, block_ids, block_counts, w_in, b_in, w_out, b_out):
    slot_rows = bound_one.shape[1] // lax.axis_size("dom")
    ids = block_ids.swapaxes(3, 4)
    out_one, out_two = pack(ids, block_counts, (features, history), slot_rows)
    border_one = borders(out_one)
    panels_one = all_panels(features)
    border_two = borders(out_two)
    tiles = adj_tiles.transpose(1, 0, 2)
    agg = first_layer(tile_cols, tiles, bound_one, panels_one, border_one)
    panels_two = all_panels(agg)
    fresh, total = inside(tile_cols, tiles, w_in, b_in.reshape(1, -1), panels_two)
    out = last_layer(total, bound_two, w_out, b_out.reshape(1, -1), border_two)
    return fresh, out


def solution(mesh):
    rows = P(("dom", "blk"), None)
    placed = (
        rows,
        rows,
        P(("dom", "blk"), None, None),
        P("dom", "blk", None),
        rows,
        rows,
        P(None, "dom", "blk", None, None),
        P(None, "dom", "blk", None),
        P(),
        P(),
        P(),
        P(),
    )
    return jax.shard_map(body, mesh=mesh, in_specs=placed, out_specs=(rows, rows), check_vma=False)
```

```python
import functools

import jax
import jax.numpy as jnp
from jax import lax
from jax.experimental import pallas as pl
from jax.experimental.pallas import tpu as pltpu
from jax.sharding import PartitionSpec as P


BF16 = jnp.bfloat16
F32 = jnp.float32
VMEM = pl.BlockSpec(memory_space=pltpu.VMEM)
MIB = 1 << 20
SMEM = pl.BlockSpec(memory_space=pltpu.SMEM)


def far(array):
    return pltpu.with_memory_space_constraint(array, pltpu.HBM)


def near(array):
    return pltpu.with_memory_space_constraint(array, pltpu.VMEM)


def dot(a, b):
    return jnp.dot(a, b, preferred_element_type=F32)


def pack_kernel(*refs):
    layers, slots, n_dom = refs[0].shape[0], *refs[0].shape[-2:]
    came_refs = refs[:layers + 2]
    out_refs = refs[layers + 3:-layers - 2]
    *held_refs, sems = refs[-layers - 2:]
    held_refs.insert(2, refs[layers + 2])
    ids_ref, counts_ref, *panel_refs = held_refs
    copies = [pltpu.make_async_copy(*pair, sems.at[n]) for n, pair in enumerate(zip(came_refs, held_refs))]
    for copy in copies:
        copy.start()
    copies[0].wait()
    copies[1].wait()
    dom = lax.axis_index("dom")
    for layer in range(layers):
        copies[2 + layer].wait()
        for apart in range(1, n_dom):
            out_ref = out_refs[layer * (n_dom - 1) + apart - 1]
            rows, width = out_ref.shape[0] // slots, out_ref.shape[1]
            reader = lax.bitwise_xor(dom, apart)
            live = counts_ref[layer, 0, 0, reader]
            for slot in range(slots):
                start = pl.multiple_of(ids_ref[layer, 0, 0, slot, reader] * rows, rows)
                here = pl.ds(slot * rows, rows)

                @pl.when(slot < live)
                def _():
                    out_ref[here, :] = panel_refs[layer][pl.ds(start, rows), :]

                @pl.when(slot >= live)
                def _():
                    out_ref[here, :] = jnp.zeros((rows, width), out_ref.dtype)


def pack(ids, counts, panels, slot_rows):
    n_dom = ids.shape[-1]
    panel, *blocks = pl.pallas_call(
        pack_kernel,
        out_shape=[pltpu.VMEM(panels[0].shape, panels[0].dtype)] + [pltpu.VMEM((slot_rows, panel.shape[1]), panel.dtype) for panel in panels for _ in range(n_dom - 1)],
        in_specs=[pl.BlockSpec(memory_space=pltpu.HBM)] * (2 + len(panels)),
        out_specs=[VMEM] * (1 + len(panels) * (n_dom - 1)),
        scratch_shapes=[pltpu.SMEM(a.shape, a.dtype) for a in (ids, counts)]
        + [pltpu.VMEM(panel.shape, panel.dtype) for panel in panels[1:]]
        + [pltpu.SemaphoreType.DMA((2 + len(panels),))],
        compiler_params=pltpu.CompilerParams(vmem_limit_bytes=2 * MIB),
        name="pack",
    )(*map(far, (ids, counts, *panels)))
    return panel, *(blocks[n * (n_dom - 1):(n + 1) * (n_dom - 1)] for n in range(len(panels)))


def stack_panels(panel_refs, stack_ref):
    rows = panel_refs[0].shape[0]
    for at, panel_ref in enumerate(panel_refs):
        stack_ref[at * rows:(at + 1) * rows, :] = panel_ref[...]


def tile_rows(cols_ref, k, rows):
    apart = lax.bitwise_xor(cols_ref[0, 0, k], lax.axis_index("blk"))
    return pl.ds(pl.multiple_of(apart * rows, rows), rows)


def border_product(dom, bound_ref, border_refs, distances):
    total = None
    for border_ref, apart in zip(border_refs, distances):
        width = border_ref.shape[0]
        owner = lax.bitwise_xor(dom, apart)
        part = dot(bound_ref[:, pl.ds(pl.multiple_of(owner * width, width), width)], border_ref[...])
        total = part if total is None else total + part
    return total


def early_kernel(adj_ref, panel_ref, tiles_ref, total_ref, held_ref, sems):
    rows = panel_ref.shape[0]
    chunks = sems.shape[0]
    step = rows // chunks
    parts = [pl.ds(n * step, step) for n in range(chunks)]
    copies = [pltpu.make_async_copy(adj_ref.at[here], held_ref.at[here], sems.at[n]) for n, here in enumerate(parts)]
    for copy in copies:
        copy.start()
    for copy, here in zip(copies, parts):
        copy.wait()
        tiles_ref[here, :] = held_ref[here].reshape(step, tiles_ref.shape[1])
    total_ref[...] = dot(tiles_ref[:, :rows], panel_ref[...])


def early_part(adj, panel):
    return pl.pallas_call(
        early_kernel,
        out_shape=[pltpu.VMEM((adj.shape[0], adj.shape[1] * adj.shape[2]), BF16), pltpu.VMEM(panel.shape, F32)],
        in_specs=[pl.BlockSpec(memory_space=pltpu.HBM), VMEM],
        out_specs=[VMEM] * 2,
        scratch_shapes=[pltpu.VMEM(adj.shape, BF16), pltpu.SemaphoreType.DMA((4,))],
        compiler_params=pltpu.CompilerParams(vmem_limit_bytes=12 * MIB),
        name="early",
    )(far(adj), near(panel))


def first_kernel(n_blk, cols_ref, tiles_ref, total_ref, bound_ref, *refs):
    panel_refs, border_refs, (agg_ref, stack_ref) = refs[:n_blk], refs[n_blk:-2], refs[-2:]
    rows = agg_ref.shape[0]
    stack_panels(panel_refs, stack_ref)
    total = total_ref[...] + border_product(lax.axis_index("dom"), bound_ref, border_refs, range(1, len(border_refs) + 1))
    for k in range(1, cols_ref.shape[-1]):
        total = total + dot(tiles_ref[:, k * rows:(k + 1) * rows], stack_ref[tile_rows(cols_ref, k, rows), :])
    agg_ref[...] = total.astype(BF16)


def first_layer(cols, tiles, total, bound, panels, border):
    shape = panels[0].shape
    return pl.pallas_call(
        functools.partial(first_kernel, len(panels)),
        out_shape=pltpu.VMEM(shape, BF16),
        in_specs=[SMEM] + [VMEM] * (3 + len(panels) + len(border)),
        out_specs=VMEM,
        scratch_shapes=[pltpu.VMEM((len(panels) * shape[0], shape[1]), BF16)],
        compiler_params=pltpu.CompilerParams(vmem_limit_bytes=8 * MIB),
        name="first",
    )(cols, *map(near, (tiles, total, bound, *panels, *border)))


def hidden(agg, w_ref, b_ref):
    return jnp.maximum(dot(agg, w_ref[...]) + b_ref[...], 0.0).astype(BF16)


def own_kernel(distances, tiles_ref, w_ref, b_ref, agg_ref, bound_ref, *refs):
    border_refs, (fresh_ref, total_ref) = refs[:-2], refs[-2:]
    fresh = hidden(agg_ref[...], w_ref, b_ref)
    fresh_ref[...] = fresh
    total = dot(tiles_ref[:, :fresh.shape[0]], fresh)
    if distances:
        total = total + border_product(lax.axis_index("dom"), bound_ref, border_refs, distances)
    total_ref[...] = total


def own_part(tiles, w_in, b_in, agg, bound, border):
    shape = (agg.shape[0], w_in.shape[1])
    return pl.pallas_call(
        functools.partial(own_kernel, tuple(border)),
        out_shape=[jax.ShapeDtypeStruct(shape, BF16), pltpu.VMEM(shape, F32)],
        in_specs=[VMEM] * (5 + len(border)),
        out_specs=[VMEM] * 2,
        compiler_params=pltpu.CompilerParams(vmem_limit_bytes=6 * MIB),
        name="own",
    )(*map(near, (tiles, w_in, b_in, agg, bound, *border.values())))


def others_kernel(n_blk, distances, cols_ref, tiles_ref, w_ref, b_ref, total_ref, bound_ref, *refs):
    panel_refs, border_refs = refs[:n_blk], refs[n_blk:-3]
    sum_ref, stack_ref, fresh_ref = refs[-3:]
    rows = panel_refs[0].shape[0]
    stack_panels(panel_refs, stack_ref)
    for k in range(1, cols_ref.shape[-1]):
        fresh_ref[(k - 1) * rows:k * rows, :] = hidden(stack_ref[tile_rows(cols_ref, k, rows), :], w_ref, b_ref)
    total = total_ref[...] + dot(tiles_ref[:, rows:], fresh_ref[...])
    if distances:
        total = total + border_product(lax.axis_index("dom"), bound_ref, border_refs, distances)
    sum_ref[...] = total


def others_part(cols, tiles, w_in, b_in, total, bound, panels, border):
    rows, width = panels[0].shape
    return pl.pallas_call(
        functools.partial(others_kernel, len(panels), tuple(border)),
        out_shape=pltpu.VMEM(total.shape, F32),
        in_specs=[SMEM] + [VMEM] * (5 + len(panels) + len(border)),
        out_specs=VMEM,
        scratch_shapes=[
            pltpu.VMEM((len(panels) * rows, width), BF16),
            pltpu.VMEM((tiles.shape[1] - rows, total.shape[1]), BF16),
        ],
        compiler_params=pltpu.CompilerParams(vmem_limit_bytes=16 * MIB),
        name="others",
    )(cols, *map(near, (tiles, w_in, b_in, total, bound, *panels, *border.values())))


def last_kernel(distances, total_ref, bound_ref, w_ref, b_ref, *refs):
    border_refs = refs[:len(distances)]
    out_ref, held_ref, sems = refs[len(distances):]
    dom = lax.axis_index("dom")
    chunks = sems.shape[0]
    rows = total_ref.shape[0] // chunks
    copies = []
    for n in range(chunks):
        here = pl.ds(n * rows, rows)
        total = total_ref[here, :] + border_product(dom, bound_ref.at[here, :], border_refs, distances)
        held_ref[here, :] = (dot(total.astype(BF16), w_ref[...]) + b_ref[...]).astype(BF16)
        copies.append(pltpu.make_async_copy(held_ref.at[here, :], out_ref.at[here, :], sems.at[n]))
        copies[n].start()
    for copy in copies:
        copy.wait()


def last_layer(total, bound, w_out, b_out, border):
    shape = (total.shape[0], w_out.shape[1])
    return pl.pallas_call(
        functools.partial(last_kernel, tuple(border)),
        out_shape=jax.ShapeDtypeStruct(shape, BF16),
        in_specs=[VMEM] * (4 + len(border)),
        out_specs=pl.BlockSpec(memory_space=pltpu.HBM),
        scratch_shapes=[pltpu.VMEM(shape, BF16), pltpu.SemaphoreType.DMA((2,))],
        compiler_params=pltpu.CompilerParams(vmem_limit_bytes=6 * MIB),
        name="last",
    )(*map(near, (total, bound, w_out, b_out, *border.values())))


def swap(block, axis, apart):
    return lax.ppermute(block, axis, [(i, i ^ apart) for i in range(lax.axis_size(axis))])


def all_panels(panel):
    n_blk = lax.axis_size("blk")
    panels = {0: panel}
    far = range(2, n_blk, 2)
    for d in (1, *far):
        panels[d] = swap(panel, "blk", d)
    for d in far:
        panels[d + 1] = swap(panels[d], "blk", 1)
    return [panels[d] for d in range(n_blk)]


def borders(blocks):
    return [swap(block, "dom", apart) for apart, block in enumerate(blocks, 1)]


def body(features, history, adj_tiles, tile_cols, bound_one, bound_two, block_ids, block_counts, w_in, b_in, w_out, b_out):
    slot_rows = bound_one.shape[1] // lax.axis_size("dom")
    ids = block_ids.swapaxes(3, 4)
    b_in, b_out = b_in.reshape(1, -1), b_out.reshape(1, -1)
    features, out_one, out_two = pack(ids, block_counts, (features, history), slot_rows)
    border_one = borders(out_one)
    panels_one = all_panels(features)
    border_two = borders(out_two)
    tiles, total = early_part(adj_tiles, features)
    agg = first_layer(tile_cols, tiles, total, bound_one, panels_one, border_one)
    panels_two = all_panels(agg)
    border_two = dict(enumerate(border_two, 1))
    soon, late = ({d: border_two[d] for d in distances} for distances in soon_and_late(len(border_two) + 1))
    rest = {d: block for d, block in border_two.items() if d not in soon and d not in late}
    fresh, total = own_part(tiles, w_in, b_in, agg, bound_two, soon)
    total = others_part(tile_cols, tiles, w_in, b_in, total, bound_two, panels_two, rest)
    out = last_layer(total, bound_two, w_out, b_out, late)
    return fresh, out


def soon_and_late(n_dom):
    return [], [1, *range(3, n_dom)]


def solution(mesh):
    rows = P(("dom", "blk"), None)
    placed = (
        rows,
        rows,
        P(("dom", "blk"), None, None),
        P("dom", "blk", None),
        rows,
        rows,
        P(None, "dom", "blk", None, None),
        P(None, "dom", "blk", None),
        P(),
        P(),
        P(),
        P(),
    )
    return jax.shard_map(body, mesh=mesh, in_specs=placed, out_specs=(rows, rows), check_vma=False)
```

```python
import functools

import jax
import jax.numpy as jnp
from jax import lax
from jax.experimental import pallas as pl
from jax.experimental.pallas import tpu as pltpu
from jax.sharding import PartitionSpec as P


BF16 = jnp.bfloat16
F32 = jnp.float32
VMEM = pl.BlockSpec(memory_space=pltpu.VMEM)
MIB = 1 << 20
SMEM = pl.BlockSpec(memory_space=pltpu.SMEM)


def far(array):
    return pltpu.with_memory_space_constraint(array, pltpu.HBM)


def near(array):
    return pltpu.with_memory_space_constraint(array, pltpu.VMEM)


def dot(a, b):
    return jnp.dot(a, b, preferred_element_type=F32)


def pack_kernel(*refs):
    layers, slots, n_dom = refs[0].shape[0], *refs[0].shape[-2:]
    came_refs = refs[:layers + 2]
    out_refs = refs[layers + 3:-layers - 2]
    *held_refs, sems = refs[-layers - 2:]
    held_refs.insert(2, refs[layers + 2])
    ids_ref, counts_ref, *panel_refs = held_refs
    copies = [pltpu.make_async_copy(*pair, sems.at[n]) for n, pair in enumerate(zip(came_refs, held_refs))]
    for copy in copies:
        copy.start()
    copies[0].wait()
    copies[1].wait()
    dom = lax.axis_index("dom")
    for layer in range(layers):
        copies[2 + layer].wait()
        for apart in range(1, n_dom):
            out_ref = out_refs[layer * (n_dom - 1) + apart - 1]
            rows, width = out_ref.shape[0] // slots, out_ref.shape[1]
            reader = lax.bitwise_xor(dom, apart)
            live = counts_ref[layer, 0, 0, reader]
            for slot in range(slots):
                start = pl.multiple_of(ids_ref[layer, 0, 0, slot, reader] * rows, rows)
                here = pl.ds(slot * rows, rows)

                @pl.when(slot < live)
                def _():
                    out_ref[here, :] = panel_refs[layer][pl.ds(start, rows), :]

                @pl.when(slot >= live)
                def _():
                    out_ref[here, :] = jnp.zeros((rows, width), out_ref.dtype)


def pack(ids, counts, panels, slot_rows):
    n_dom = ids.shape[-1]
    panel, *blocks = pl.pallas_call(
        pack_kernel,
        out_shape=[pltpu.VMEM(panels[0].shape, panels[0].dtype)] + [pltpu.VMEM((slot_rows, panel.shape[1]), panel.dtype) for panel in panels for _ in range(n_dom - 1)],
        in_specs=[pl.BlockSpec(memory_space=pltpu.HBM)] * (2 + len(panels)),
        out_specs=[VMEM] * (1 + len(panels) * (n_dom - 1)),
        scratch_shapes=[pltpu.SMEM(a.shape, a.dtype) for a in (ids, counts)]
        + [pltpu.VMEM(panel.shape, panel.dtype) for panel in panels[1:]]
        + [pltpu.SemaphoreType.DMA((2 + len(panels),))],
        compiler_params=pltpu.CompilerParams(vmem_limit_bytes=2 * MIB),
        name="pack",
    )(*map(far, (ids, counts, *panels)))
    return panel, *(blocks[n * (n_dom - 1):(n + 1) * (n_dom - 1)] for n in range(len(panels)))


def stack_panels(panel_refs, stack_ref):
    rows = panel_refs[0].shape[0]
    for at, panel_ref in enumerate(panel_refs):
        stack_ref[at * rows:(at + 1) * rows, :] = panel_ref[...]


def tile_rows(cols_ref, k, rows):
    apart = lax.bitwise_xor(cols_ref[0, 0, k], lax.axis_index("blk"))
    return pl.ds(pl.multiple_of(apart * rows, rows), rows)


def border_product(dom, bound_ref, border_refs, distances):
    total = None
    for border_ref, apart in zip(border_refs, distances):
        width = border_ref.shape[0]
        owner = lax.bitwise_xor(dom, apart)
        part = dot(bound_ref[:, pl.ds(pl.multiple_of(owner * width, width), width)], border_ref[...])
        total = part if total is None else total + part
    return total


def early_kernel(adj_ref, panel_ref, tiles_ref, total_ref, held_ref, sems):
    rows = panel_ref.shape[0]
    chunks = sems.shape[0]
    step = rows // chunks
    parts = [pl.ds(n * step, step) for n in range(chunks)]
    copies = [pltpu.make_async_copy(adj_ref.at[here], held_ref.at[here], sems.at[n]) for n, here in enumerate(parts)]
    for copy in copies:
        copy.start()
    for copy, here in zip(copies, parts):
        copy.wait()
        tiles_ref[here, :] = held_ref[here].reshape(step, tiles_ref.shape[1])
    total_ref[...] = dot(tiles_ref[:, :rows], panel_ref[...])


def early_part(adj, panel):
    return pl.pallas_call(
        early_kernel,
        out_shape=[pltpu.VMEM((adj.shape[0], adj.shape[1] * adj.shape[2]), BF16), pltpu.VMEM(panel.shape, F32)],
        in_specs=[pl.BlockSpec(memory_space=pltpu.HBM), VMEM],
        out_specs=[VMEM] * 2,
        scratch_shapes=[pltpu.VMEM(adj.shape, BF16), pltpu.SemaphoreType.DMA((8,))],
        compiler_params=pltpu.CompilerParams(vmem_limit_bytes=12 * MIB),
        name="early",
    )(far(adj), near(panel))


def first_kernel(n_blk, cols_ref, tiles_ref, total_ref, bound_ref, *refs):
    panel_refs, border_refs, (agg_ref, stack_ref) = refs[:n_blk], refs[n_blk:-2], refs[-2:]
    rows = agg_ref.shape[0]
    stack_panels(panel_refs, stack_ref)
    total = total_ref[...] + border_product(lax.axis_index("dom"), bound_ref, border_refs, range(1, len(border_refs) + 1))
    for k in range(1, cols_ref.shape[-1]):
        total = total + dot(tiles_ref[:, k * rows:(k + 1) * rows], stack_ref[tile_rows(cols_ref, k, rows), :])
    agg_ref[...] = total.astype(BF16)


def first_layer(cols, tiles, total, bound, panels, border):
    shape = panels[0].shape
    return pl.pallas_call(
        functools.partial(first_kernel, len(panels)),
        out_shape=pltpu.VMEM(shape, BF16),
        in_specs=[SMEM] + [VMEM] * (3 + len(panels) + len(border)),
        out_specs=VMEM,
        scratch_shapes=[pltpu.VMEM((len(panels) * shape[0], shape[1]), BF16)],
        compiler_params=pltpu.CompilerParams(vmem_limit_bytes=8 * MIB),
        name="first",
    )(cols, *map(near, (tiles, total, bound, *panels, *border)))


def hidden(agg, w_ref, b_ref):
    return jnp.maximum(dot(agg, w_ref[...]) + b_ref[...], 0.0).astype(BF16)


def own_kernel(distances, tiles_ref, w_ref, b_ref, agg_ref, bound_ref, *refs):
    border_refs, (fresh_ref, total_ref) = refs[:-2], refs[-2:]
    fresh = hidden(agg_ref[...], w_ref, b_ref)
    fresh_ref[...] = fresh
    total = dot(tiles_ref[:, :fresh.shape[0]], fresh)
    if distances:
        total = total + border_product(lax.axis_index("dom"), bound_ref, border_refs, distances)
    total_ref[...] = total


def own_part(tiles, w_in, b_in, agg, bound, border):
    shape = (agg.shape[0], w_in.shape[1])
    return pl.pallas_call(
        functools.partial(own_kernel, tuple(border)),
        out_shape=[jax.ShapeDtypeStruct(shape, BF16), pltpu.VMEM(shape, F32)],
        in_specs=[VMEM] * (5 + len(border)),
        out_specs=[VMEM] * 2,
        compiler_params=pltpu.CompilerParams(vmem_limit_bytes=6 * MIB),
        name="own",
    )(*map(near, (tiles, w_in, b_in, agg, bound, *border.values())))


def others_kernel(n_blk, distances, cols_ref, tiles_ref, w_ref, b_ref, total_ref, bound_ref, *refs):
    panel_refs, border_refs = refs[:n_blk], refs[n_blk:-3]
    sum_ref, stack_ref, fresh_ref = refs[-3:]
    rows = panel_refs[0].shape[0]
    stack_panels(panel_refs, stack_ref)
    for k in range(1, cols_ref.shape[-1]):
        fresh_ref[(k - 1) * rows:k * rows, :] = hidden(stack_ref[tile_rows(cols_ref, k, rows), :], w_ref, b_ref)
    total = total_ref[...] + dot(tiles_ref[:, rows:], fresh_ref[...])
    if distances:
        total = total + border_product(lax.axis_index("dom"), bound_ref, border_refs, distances)
    sum_ref[...] = total


def others_part(cols, tiles, w_in, b_in, total, bound, panels, border):
    rows, width = panels[0].shape
    return pl.pallas_call(
        functools.partial(others_kernel, len(panels), tuple(border)),
        out_shape=pltpu.VMEM(total.shape, F32),
        in_specs=[SMEM] + [VMEM] * (5 + len(panels) + len(border)),
        out_specs=VMEM,
        scratch_shapes=[
            pltpu.VMEM((len(panels) * rows, width), BF16),
            pltpu.VMEM((tiles.shape[1] - rows, total.shape[1]), BF16),
        ],
        compiler_params=pltpu.CompilerParams(vmem_limit_bytes=16 * MIB),
        name="others",
    )(cols, *map(near, (tiles, w_in, b_in, total, bound, *panels, *border.values())))


def last_kernel(distances, total_ref, bound_ref, w_ref, b_ref, *refs):
    border_refs = refs[:len(distances)]
    out_ref, held_ref, sems = refs[len(distances):]
    dom = lax.axis_index("dom")
    total = (total_ref[...] + border_product(dom, bound_ref, border_refs, distances)).astype(BF16)
    chunks = sems.shape[0]
    rows = total_ref.shape[0] // chunks
    copies = []
    for n in range(chunks):
        here = pl.ds(n * rows, rows)
        held_ref[here, :] = (dot(total[n * rows:(n + 1) * rows], w_ref[...]) + b_ref[...]).astype(BF16)
        copies.append(pltpu.make_async_copy(held_ref.at[here, :], out_ref.at[here, :], sems.at[n]))
        copies[n].start()
    for copy in copies:
        copy.wait()


def last_layer(total, bound, w_out, b_out, border):
    shape = (total.shape[0], w_out.shape[1])
    return pl.pallas_call(
        functools.partial(last_kernel, tuple(border)),
        out_shape=jax.ShapeDtypeStruct(shape, BF16),
        in_specs=[VMEM] * (4 + len(border)),
        out_specs=pl.BlockSpec(memory_space=pltpu.HBM),
        scratch_shapes=[pltpu.VMEM(shape, BF16), pltpu.SemaphoreType.DMA((4,))],
        compiler_params=pltpu.CompilerParams(vmem_limit_bytes=6 * MIB),
        name="last",
    )(*map(near, (total, bound, w_out, b_out, *border.values())))


def swap(block, axis, apart):
    return lax.ppermute(block, axis, [(i, i ^ apart) for i in range(lax.axis_size(axis))])


def all_panels(panel):
    n_blk = lax.axis_size("blk")
    panels = {0: panel}
    far = range(2, n_blk, 2)
    for d in (1, *far):
        panels[d] = swap(panel, "blk", d)
    for d in far:
        panels[d + 1] = swap(panels[d], "blk", 1)
    return [panels[d] for d in range(n_blk)]


def borders(blocks):
    return [swap(block, "dom", apart) for apart, block in enumerate(blocks, 1)]


def body(features, history, adj_tiles, tile_cols, bound_one, bound_two, block_ids, block_counts, w_in, b_in, w_out, b_out):
    slot_rows = bound_one.shape[1] // lax.axis_size("dom")
    ids = block_ids.swapaxes(3, 4)
    b_in, b_out = b_in.reshape(1, -1), b_out.reshape(1, -1)
    features, out_one, out_two = pack(ids, block_counts, (features, history), slot_rows)
    border_one = borders(out_one)
    panels_one = all_panels(features)
    border_two = borders(out_two)
    tiles, total = early_part(adj_tiles, features)
    agg = first_layer(tile_cols, tiles, total, bound_one, panels_one, border_one)
    panels_two = all_panels(agg)
    border_two = dict(enumerate(border_two, 1))
    soon, late = ({d: border_two[d] for d in distances} for distances in soon_and_late(len(border_two) + 1))
    rest = {d: block for d, block in border_two.items() if d not in soon and d not in late}
    fresh, total = own_part(tiles, w_in, b_in, agg, bound_two, soon)
    total = others_part(tile_cols, tiles, w_in, b_in, total, bound_two, panels_two, rest)
    out = last_layer(total, bound_two, w_out, b_out, late)
    return fresh, out


def soon_and_late(n_dom):
    return [], [1, *range(3, n_dom)]


def solution(mesh):
    rows = P(("dom", "blk"), None)
    placed = (
        rows,
        rows,
        P(("dom", "blk"), None, None),
        P("dom", "blk", None),
        rows,
        rows,
        P(None, "dom", "blk", None, None),
        P(None, "dom", "blk", None),
        P(),
        P(),
        P(),
        P(),
    )
    return jax.shard_map(body, mesh=mesh, in_specs=placed, out_specs=(rows, rows), check_vma=False)
```
